256 devices in a mesh: dp: 4 (over y_lo, core), tm: 4 (over x), rows: 16 (over z, y_hi).
Axes of the slice: x: 4, y: 4 (y_hi: 2, y_lo: 2; y = y_hi * 2 + y_lo), z: 8, core: 2. Of those that a mesh axis runs over, the one named last changes fastest.
Arguments:
- latents: bfloat16 [4, 8, 16, 30, 512], P('dp', 'tm', 'rows'), may hold values from -6 to 6
- grad_out: bfloat16 [4, 8, 32, 60, 256], P('dp', 'tm', 'rows'), may hold values from -6 to 6
- kernel: bfloat16 [3, 3, 3, 512, 256], replicated, may hold values from -0.0546875 to 0.0546875
Outputs:
- grad_latents: bfloat16 [4, 8, 16, 30, 512], P('dp', 'tm', 'rows')
- weight_grad: float32 [512, 3, 3, 3, 256], P(('dp', 'tm', 'rows'))
The draws below stay inside these ranges and needn't reach their ends.
All inputs are finite; a program needn't handle non-finite values.
Results may differ from the reference program's by a relative error of at most 0.001.
Values may be sent and summed in bfloat16 or wider, within the bound.
A program may use at most 128 MiB of HBM per device.

```python
import jax
import jax.numpy as jnp
from jax import lax

CIN = 512
COUT = 256
WL = 30
CLIPS = 4
FRAMES = 8
HL = 16
HUP = 32
WUP = 60


def with_spikes(values, stream_key, source, target, blocks, factor):
    owner, partner = [(jnp.arange(values.shape[axis_at]) // (values.shape[axis_at] // blocks)).reshape([-1 if axis == axis_at else 1 for axis in range(values.ndim)]) for axis_at in (source, target)]
    chosen = jax.random.permutation(stream_key, blocks)[partner]
    strong = (owner == chosen) | (owner == (partner + blocks // 2) % blocks)
    return jnp.where(strong, factor * values, values)


def block_scale(own_key, shape, shards, least, top_value):
    level, own = 1.0, jax.random.fold_in(own_key, 6)
    for dim, blocks in shards:
        draws = jnp.exp(jax.random.uniform(jax.random.fold_in(own, dim), (blocks,), jnp.float32, least / len(shards), top_value / len(shards)))
        level = level * jnp.repeat(draws, shape[dim] // blocks).reshape([-1 if axis == dim else 1 for axis in range(len(shape))])
    return level


def bell_draw(key, dims, deviation, reach, split=(), held_as=jnp.bfloat16):
    entries = deviation * jax.random.normal(key, dims, jnp.float32)
    if split:
        entries = entries * block_scale(key, dims, split, -0.22, 0.18)
    return jnp.clip(entries, -reach, reach).astype(held_as)


def heavy_noise(own_key, extent, spread, reach, cuts, heavy, dtype=jnp.bfloat16):
    result = spread * jax.random.normal(own_key, extent, jnp.float32)
    if cuts:
        result = result * block_scale(own_key, extent, cuts, -0.22, 0.18)
    return jnp.clip(with_spikes(result, jax.random.fold_in(own_key, 3), *heavy), -reach, reach).astype(dtype)


def setup_inputs(seed: int = 0) -> dict:
    streams_of = jax.random.split(jax.random.key(seed), 4)
    return {
        "latents": heavy_noise(streams_of[0], (CLIPS, FRAMES, HL, WL, CIN), 1.0, 6.0, ((0, 4), (1, 4), (2, 16)), (2, 4, 16, 2.0)),
        "grad_out": bell_draw(streams_of[1], (CLIPS, FRAMES, HUP, WUP, COUT), 1.0, 6.0, ((0, 4), (1, 4), (2, 16))),
        "kernel": bell_draw(streams_of[2], (3, 3, 3, CIN, COUT), (27 * CIN) ** -0.5, 0.0546875),
    }


def reference(latents, grad_out, kernel):
    frames = grad_out.shape[1]
    height = grad_out.shape[2]
    width = grad_out.shape[3]
    count = grad_out.shape[0] * frames * height * width
    factor = float(count) ** -0.5
    kernel_full = kernel.astype(jnp.float32)

    def one_clip(pair):
        clip, grad = pair
        grad_full = grad.astype(jnp.float32)
        upsampled = jnp.repeat(jnp.repeat(clip.astype(jnp.float32), 2, axis=1), 2, axis=2)
        up_pad = jnp.pad(upsampled, ((2, 0), (1, 1), (1, 1), (0, 0)))
        grad_pad = jnp.pad(grad_full, ((0, 2), (1, 1), (1, 1), (0, 0)))
        grad_up = jnp.zeros(upsampled.shape, jnp.float32)
        taps = []
        for a in range(3):
            for i in range(3):
                for j in range(3):
                    window = grad_pad[2 - a:2 - a + frames, 2 - i:2 - i + height, 2 - j:2 - j + width]
                    grad_up = grad_up + jnp.einsum("fhwo,co->fhwc", window, kernel_full[a, i, j], precision=lax.Precision.HIGHEST)
                    source = up_pad[a:a + frames, i:i + height, j:j + width]
                    taps.append(jnp.einsum("fhwc,fhwo->co", source, grad_full, precision=lax.Precision.HIGHEST))
        channels = grad_up.shape[3]
        pooled = grad_up.reshape(frames, height // 2, 2, width // 2, 2, channels).sum(axis=(2, 4))
        return pooled.astype(jnp.bfloat16), jnp.stack(taps, axis=1)

    grad_latents, terms = lax.map(one_clip, (latents, grad_out))
    summed = jnp.sum(terms, axis=0) * factor
    weight_grad = summed.reshape(summed.shape[0], 3, 3, 3, summed.shape[2])
    return grad_latents, weight_grad
```

```python
import jax
import jax.numpy as jnp
from jax import lax
from jax.sharding import PartitionSpec as P


def shift_from(shard, axis, by):
    peers = lax.axis_size(axis)
    pairs = [(i, i + by) for i in range(peers) if 0 <= i + by < peers]
    return lax.ppermute(shard, axis, pairs)


def pool_pairs(values, dim):
    n = values.shape[dim] // 2
    pad = [(0, 0)] * values.ndim
    pad[dim] = (1, 1)
    ext = jnp.pad(values, pad)
    out = []
    for i in range(3):
        start = 2 - i
        a = lax.slice_in_dim(ext, start, start + 2 * n - 1, stride=2, axis=dim)
        b = lax.slice_in_dim(ext, start + 1, start + 2 * n, stride=2, axis=dim)
        out.append(a + b)
    return jnp.stack(out, axis=dim + 1)


def body(latents, grad_out, kernel):
    frames = grad_out.shape[1]
    height = grad_out.shape[2]
    width = grad_out.shape[3]
    channels = latents.shape[4]
    outputs = grad_out.shape[4]
    devices = lax.axis_size("dp") * lax.axis_size("tm") * lax.axis_size("rows")
    factor = float(devices * frames * height * width) ** (-0.5)
    slab_count = lax.axis_size("rows")
    slab = lax.axis_index("rows")

    grad_whole = lax.all_gather(grad_out[0], "rows", axis=1, tiled=True)
    whole_height = grad_whole.shape[1]

    padded_rows = jnp.pad(grad_whole, ((0, 0), (1, 1), (0, 0), (0, 0)))
    near = lax.dynamic_slice_in_dim(padded_rows, slab * height, height + 2, axis=1)
    later = shift_from(near, "tm", -1)
    grad_all = jnp.concatenate([near, later], axis=0)
    grad_all = jnp.pad(grad_all, ((0, 0), (0, 0), (1, 1), (0, 0)))
    patches = []
    for a in range(3):
        for i in range(3):
            for j in range(3):
                patches.append(
                    grad_all[2 - a : 2 - a + frames, 2 - i : 2 - i + height, 2 - j : 2 - j + width]
                )
    patches = jnp.stack(patches, axis=3).reshape(frames * height * width, 27, outputs)
    grad_up = lax.dot_general(
        patches,
        kernel.reshape(27, channels, outputs),
        (((1, 2), (0, 2)), ((), ())),
        preferred_element_type=jnp.float32,
    )
    pooled = grad_up.reshape(frames, height // 2, 2, width // 2, 2, channels).sum(axis=(2, 4))
    grad_latents = pooled.astype(jnp.bfloat16)[None]

    groups = lax.axis_size("dp") * lax.axis_size("tm")
    share = channels // devices
    earlier = shift_from(latents, "tm", 1)
    with_earlier = jnp.concatenate([earlier, latents], axis=1)
    lead = with_earlier.shape[:4]
    regrouped = with_earlier.reshape(lead + (groups, slab_count, share))
    regrouped = jnp.swapaxes(regrouped, 4, 5).reshape(lead + (channels,))
    owned = lax.all_to_all(regrouped, "rows", split_axis=4, concat_axis=2, tiled=True)[0]
    group_channels = owned.shape[3]
    taps_a = jnp.stack([owned[a : a + frames] for a in range(3)], axis=0)

    pooled_grad = pool_pairs(pool_pairs(grad_whole.astype(jnp.float32), 1), 3)
    scaled = pooled_grad * 65537.0
    top = scaled - (scaled - pooled_grad)
    both = jnp.stack([top, pooled_grad - top], axis=0).astype(jnp.bfloat16)
    term = jnp.einsum(
        "afrsc,xfrisjo->caijxo", taps_a, both, preferred_element_type=jnp.float32
    )
    term = (term[..., 0, :] + term[..., 1, :]) * factor
    term = term.reshape(group_channels, 3, 3, 3, outputs)
    term = lax.psum_scatter(term, "dp", scatter_dimension=0, tiled=True)
    weight_grad = lax.psum_scatter(term, "tm", scatter_dimension=0, tiled=True)
    return (grad_latents, weight_grad)


def solution(mesh):
    in_specs = (P("dp", "tm", "rows", None, None), P("dp", "tm", "rows", None, None), P())
    out_specs = (P("dp", "tm", "rows", None, None), P(("dp", "tm", "rows"), None, None, None, None))
    return jax.shard_map(body, mesh=mesh, in_specs=in_specs, out_specs=out_specs, check_vma=False)
```

```python
import jax
import jax.numpy as jnp
from jax import lax
from jax.sharding import PartitionSpec as P


def shift_from(shard, axis, by):
    peers = lax.axis_size(axis)
    pairs = [(i, i + by) for i in range(peers) if 0 <= i + by < peers]
    return lax.ppermute(shard, axis, pairs)


def pool_pairs(values, dim):
    n = values.shape[dim] // 2
    pad = [(0, 0)] * values.ndim
    pad[dim] = (1, 1)
    ext = jnp.pad(values, pad)
    shape = values.shape
    shifted = ext.reshape(shape[:dim] + (n + 1, 2) + shape[dim + 1 :]).sum(axis=dim + 1)
    aligned = values.reshape(shape[:dim] + (n, 2) + shape[dim + 1 :]).sum(axis=dim + 1)
    out = [
        lax.slice_in_dim(shifted, 1, n + 1, axis=dim),
        aligned,
        lax.slice_in_dim(shifted, 0, n, axis=dim),
    ]
    return jnp.stack(out, axis=dim + 1)


def with_halo(block, axis, dim, width):
    count = lax.axis_size(axis)
    forward = [(i, i + 1) for i in range(count - 1)]
    backward = [(target, source) for source, target in forward]
    low = lax.ppermute(
        lax.slice_in_dim(block, block.shape[dim] - width, None, axis=dim), axis, forward
    )
    high = lax.ppermute(lax.slice_in_dim(block, 0, width, axis=dim), axis, backward)
    return jnp.concatenate([low, block, high], axis=dim)


def body(latents, grad_out, kernel):
    frames = grad_out.shape[1]
    height = grad_out.shape[2]
    width = grad_out.shape[3]
    channels = latents.shape[4]
    outputs = grad_out.shape[4]
    devices = lax.axis_size("dp") * lax.axis_size("tm") * lax.axis_size("rows")
    factor = float(devices * frames * height * width) ** (-0.5)
    slab_count = lax.axis_size("rows")

    grad_whole = lax.all_gather(grad_out[0], "rows", axis=1, tiled=True)
    whole_height = grad_whole.shape[1]

    near = with_halo(grad_out[0], "rows", 1, 1)
    later = shift_from(near, "tm", -1)
    grad_all = jnp.concatenate([near, later], axis=0)
    grad_all = jnp.pad(grad_all, ((0, 0), (0, 0), (1, 1), (0, 0)))
    patches = []
    for a in range(3):
        for i in range(3):
            for j in range(3):
                patches.append(
                    grad_all[2 - a : 2 - a + frames, 2 - i : 2 - i + height, 2 - j : 2 - j + width]
                )
    patches = jnp.stack(patches, axis=3).reshape(frames * height * width, 27, outputs)
    grad_up = lax.dot_general(
        patches,
        kernel.reshape(27, channels, outputs),
        (((1, 2), (0, 2)), ((), ())),
        preferred_element_type=jnp.float32,
    )
    pooled = grad_up.reshape(frames, height // 2, 2, width // 2, 2, channels).sum(axis=(2, 4))
    grad_latents = pooled.astype(jnp.bfloat16)[None]

    groups = lax.axis_size("dp") * lax.axis_size("tm")
    share = channels // devices
    earlier = shift_from(latents, "tm", 1)
    with_earlier = jnp.concatenate([earlier, latents], axis=1)
    lead = with_earlier.shape[:4]
    regrouped = with_earlier.reshape(lead + (groups, slab_count, share))
    regrouped = jnp.swapaxes(regrouped, 4, 5).reshape(lead + (channels,))
    owned = lax.all_to_all(regrouped, "rows", split_axis=4, concat_axis=2, tiled=True)[0]
    group_channels = owned.shape[3]
    taps_a = jnp.stack([owned[a : a + frames] for a in range(3)], axis=0)

    pooled_grad = pool_pairs(pool_pairs(grad_whole.astype(jnp.float32), 1), 3)
    scaled = pooled_grad * 65537.0
    top = scaled - (scaled - pooled_grad)
    both = jnp.stack([top, pooled_grad - top], axis=0).astype(jnp.bfloat16)
    term = jnp.einsum(
        "afrsc,xfrisjo->caijxo", taps_a, both, preferred_element_type=jnp.float32
    )
    term = (term[..., 0, :] + term[..., 1, :]) * factor
    term = term.reshape(group_channels, 3, 3, 3, outputs)
    term = lax.psum_scatter(term, "dp", scatter_dimension=0, tiled=True)
    weight_grad = lax.psum_scatter(term, "tm", scatter_dimension=0, tiled=True)
    return (grad_latents, weight_grad)


def solution(mesh):
    in_specs = (P("dp", "tm", "rows", None, None), P("dp", "tm", "rows", None, None), P())
    out_specs = (P("dp", "tm", "rows", None, None), P(("dp", "tm", "rows"), None, None, None, None))
    return jax.shard_map(body, mesh=mesh, in_specs=in_specs, out_specs=out_specs, check_vma=False)
```

```python
import jax
import jax.numpy as jnp
from jax import lax
from jax.sharding import PartitionSpec as P
from jax.experimental import pallas as pl
from jax.experimental.pallas import tpu as pltpu


def shift_from(shard, axis, by):
    peers = lax.axis_size(axis)
    pairs = [(i, i + by) for i in range(peers) if 0 <= i + by < peers]
    return lax.ppermute(shard, axis, pairs)


def pool_pairs(values, dim):
    n = values.shape[dim] // 2
    pad = [(0, 0)] * values.ndim
    pad[dim] = (1, 1)
    ext = jnp.pad(values, pad)
    shape = values.shape
    shifted = ext.reshape(shape[:dim] + (n + 1, 2) + shape[dim + 1 :]).sum(axis=dim + 1)
    aligned = values.reshape(shape[:dim] + (n, 2) + shape[dim + 1 :]).sum(axis=dim + 1)
    out = [
        lax.slice_in_dim(shifted, 1, n + 1, axis=dim),
        aligned,
        lax.slice_in_dim(shifted, 0, n, axis=dim),
    ]
    return jnp.stack(out, axis=dim + 1)


def with_halo(block, axis, dim, width):
    count = lax.axis_size(axis)
    forward = [(i, i + 1) for i in range(count - 1)]
    backward = [(target, source) for source, target in forward]
    low = lax.ppermute(
        lax.slice_in_dim(block, block.shape[dim] - width, None, axis=dim), axis, forward
    )
    high = lax.ppermute(lax.slice_in_dim(block, 0, width, axis=dim), axis, backward)
    return jnp.concatenate([low, block, high], axis=dim)


def scatter_sum_kernel(term_ref, out_ref, slots, send_sem, recv_sem):
    tm_size = lax.axis_size("tm")
    count = lax.axis_size("dp") * tm_size
    row = lax.axis_index("rows")
    me = lax.axis_index("dp") * tm_size + lax.axis_index("tm")
    mesh_id = pl.DeviceIdType.MESH

    def device(k):
        return (k // tm_size, k % tm_size, row)

    barrier = pltpu.get_barrier_semaphore()
    for d in range(1, count):
        pl.semaphore_signal(barrier, inc=1, device_id=device((me + d) % count), device_id_type=mesh_id)
    pl.semaphore_wait(barrier, count - 1)

    copies = []
    for d in range(1, count):
        target = (me + d) % count
        copy = pltpu.make_async_remote_copy(
            src_ref=term_ref.at[target],
            dst_ref=slots.at[me],
            send_sem=send_sem.at[d - 1],
            recv_sem=recv_sem.at[me],
            device_id=device(target),
            device_id_type=mesh_id,
        )
        copy.start()
        copies.append(copy)
    total = term_ref[me]
    for d in range(1, count):
        source = (me + count - d) % count
        incoming = pltpu.make_async_remote_copy(
            src_ref=term_ref.at[source],
            dst_ref=slots.at[source],
            send_sem=send_sem.at[d - 1],
            recv_sem=recv_sem.at[source],
            device_id=device(source),
            device_id_type=mesh_id,
        )
        incoming.wait_recv()
        total = total + slots[source]
    out_ref[...] = total
    for copy in copies:
        copy.wait_send()


def scatter_sum(term):
    count, rows, lanes = term.shape
    return pl.pallas_call(
        scatter_sum_kernel,
        out_shape=jax.ShapeDtypeStruct((rows, lanes), term.dtype),
        in_specs=[pl.BlockSpec(memory_space=pltpu.VMEM)],
        out_specs=pl.BlockSpec(memory_space=pltpu.VMEM),
        scratch_shapes=[
            pltpu.VMEM((count, rows, lanes), term.dtype),
            pltpu.SemaphoreType.DMA((count - 1,)),
            pltpu.SemaphoreType.DMA((count,)),
        ],
        compiler_params=pltpu.CompilerParams(collective_id=0, has_side_effects=True),
    )(term)


def body(latents, grad_out, kernel):
    frames = grad_out.shape[1]
    height = grad_out.shape[2]
    width = grad_out.shape[3]
    channels = latents.shape[4]
    outputs = grad_out.shape[4]
    devices = lax.axis_size("dp") * lax.axis_size("tm") * lax.axis_size("rows")
    factor = float(devices * frames * height * width) ** (-0.5)
    slab_count = lax.axis_size("rows")

    grad_whole = lax.all_gather(grad_out[0], "rows", axis=1, tiled=True)
    whole_height = grad_whole.shape[1]

    near = with_halo(grad_out[0], "rows", 1, 1)
    later = shift_from(near, "tm", -1)
    grad_all = jnp.concatenate([near, later], axis=0)
    grad_all = jnp.pad(grad_all, ((0, 0), (0, 0), (1, 1), (0, 0)))
    patches = []
    for a in range(3):
        for i in range(3):
            for j in range(3):
                patches.append(
                    grad_all[2 - a : 2 - a + frames, 2 - i : 2 - i + height, 2 - j : 2 - j + width]
                )
    patches = jnp.stack(patches, axis=3).reshape(frames * height * width, 27, outputs)
    grad_up = lax.dot_general(
        patches,
        kernel.reshape(27, channels, outputs),
        (((1, 2), (0, 2)), ((), ())),
        preferred_element_type=jnp.float32,
    )
    pooled = grad_up.reshape(frames, height // 2, 2, width // 2, 2, channels).sum(axis=(2, 4))
    grad_latents = pooled.astype(jnp.bfloat16)[None]

    groups = lax.axis_size("dp") * lax.axis_size("tm")
    share = channels // devices
    earlier = shift_from(latents, "tm", 1)
    with_earlier = jnp.concatenate([earlier, latents], axis=1)
    lead = with_earlier.shape[:4]
    regrouped = with_earlier.reshape(lead + (groups, slab_count, share))
    regrouped = jnp.swapaxes(regrouped, 4, 5).reshape(lead + (channels,))
    owned = lax.all_to_all(regrouped, "rows", split_axis=4, concat_axis=2, tiled=True)[0]
    group_channels = owned.shape[3]
    taps_a = jnp.stack([owned[a : a + frames] for a in range(3)], axis=0)

    pooled_grad = pool_pairs(pool_pairs(grad_whole.astype(jnp.float32), 1), 3)
    scaled = pooled_grad * 65537.0
    top = scaled - (scaled - pooled_grad)
    both = jnp.stack([top, pooled_grad - top], axis=0).astype(jnp.bfloat16)
    term = jnp.einsum(
        "afrsc,xfrisjo->caijxo", taps_a, both, preferred_element_type=jnp.float32
    )
    term = (term[..., 0, :] + term[..., 1, :]) * factor
    share_size = share * 27 * outputs
    term = term.reshape(groups, share_size // 128, 128)
    weight_grad = scatter_sum(term).reshape(share, 3, 3, 3, outputs)
    return (grad_latents, weight_grad)


def solution(mesh):
    in_specs = (P("dp", "tm", "rows", None, None), P("dp", "tm", "rows", None, None), P())
    out_specs = (P("dp", "tm", "rows", None, None), P(("dp", "tm", "rows"), None, None, None, None))
    return jax.shard_map(body, mesh=mesh, in_specs=in_specs, out_specs=out_specs, check_vma=False)
```

```python
import jax
import jax.numpy as jnp
from jax import lax
from jax.sharding import PartitionSpec as P
from jax.experimental import pallas as pl
from jax.experimental.pallas import tpu as pltpu


def shift_from(shard, axis, by):
    peers = lax.axis_size(axis)
    pairs = [(i, i + by) for i in range(peers) if 0 <= i + by < peers]
    return lax.ppermute(shard, axis, pairs)


def pool_pairs(values, dim):
    n = values.shape[dim] // 2
    pad = [(0, 0)] * values.ndim
    pad[dim] = (1, 1)
    ext = jnp.pad(values, pad)
    shape = values.shape
    shifted = ext.reshape(shape[:dim] + (n + 1, 2) + shape[dim + 1 :]).sum(axis=dim + 1)
    aligned = values.reshape(shape[:dim] + (n, 2) + shape[dim + 1 :]).sum(axis=dim + 1)
    out = [
        lax.slice_in_dim(shifted, 1, n + 1, axis=dim),
        aligned,
        lax.slice_in_dim(shifted, 0, n, axis=dim),
    ]
    return jnp.stack(out, axis=dim + 1)


def with_halo(block, axis, dim, width):
    count = lax.axis_size(axis)
    forward = [(i, i + 1) for i in range(count - 1)]
    backward = [(target, source) for source, target in forward]
    low = lax.ppermute(
        lax.slice_in_dim(block, block.shape[dim] - width, None, axis=dim), axis, forward
    )
    high = lax.ppermute(lax.slice_in_dim(block, 0, width, axis=dim), axis, backward)
    return jnp.concatenate([low, block, high], axis=dim)


def scatter_sum_kernel(term_ref, out_ref, slots, send_sem, recv_sem):
    tm_size = lax.axis_size("tm")
    count = lax.axis_size("dp") * tm_size
    row = lax.axis_index("rows")
    me = lax.axis_index("dp") * tm_size + lax.axis_index("tm")
    mesh_id = pl.DeviceIdType.MESH

    def device(k):
        return (k // tm_size, k % tm_size, row)

    barrier = pltpu.get_barrier_semaphore()
    for d in range(1, count):
        pl.semaphore_signal(barrier, inc=1, device_id=device((me + d) % count), device_id_type=mesh_id)
    pl.semaphore_wait(barrier, count - 1)

    copies = []
    for d in range(1, count):
        target = (me + d) % count
        copy = pltpu.make_async_remote_copy(
            src_ref=term_ref.at[target],
            dst_ref=slots.at[me],
            send_sem=send_sem.at[d - 1],
            recv_sem=recv_sem.at[me],
            device_id=device(target),
            device_id_type=mesh_id,
        )
        copy.start()
        copies.append(copy)
    total = term_ref[me]
    for d in range(1, count):
        source = (me + count - d) % count
        incoming = pltpu.make_async_remote_copy(
            src_ref=term_ref.at[source],
            dst_ref=slots.at[source],
            send_sem=send_sem.at[d - 1],
            recv_sem=recv_sem.at[source],
            device_id=device(source),
            device_id_type=mesh_id,
        )
        incoming.wait_recv()
        total = total + slots[source]
    out_ref[...] = total
    for copy in copies:
        copy.wait_send()


def scatter_sum(term):
    count, rows, lanes = term.shape
    return pl.pallas_call(
        scatter_sum_kernel,
        out_shape=jax.ShapeDtypeStruct((rows, lanes), term.dtype),
        in_specs=[pl.BlockSpec(memory_space=pltpu.VMEM)],
        out_specs=pl.BlockSpec(memory_space=pltpu.VMEM),
        scratch_shapes=[
            pltpu.VMEM((count, rows, lanes), term.dtype),
            pltpu.SemaphoreType.DMA((count - 1,)),
            pltpu.SemaphoreType.DMA((count,)),
        ],
        compiler_params=pltpu.CompilerParams(collective_id=0, has_side_effects=True),
    )(term)


def row_exchange_kernel(grad_ref, lat_ref, grad_buf, lat_buf, send_sem, recv_sem):
    count = lax.axis_size("rows")
    me = lax.axis_index("rows")
    mesh_id = pl.DeviceIdType.MESH

    def device(k):
        return (lax.axis_index("dp"), lax.axis_index("tm"), k)

    barrier = pltpu.get_barrier_semaphore()
    for d in range(1, count):
        pl.semaphore_signal(barrier, inc=1, device_id=device((me + d) % count), device_id_type=mesh_id)
    pl.semaphore_wait(barrier, count - 1)

    def grad_copy(d, peer, slot):
        return pltpu.make_async_remote_copy(
            src_ref=grad_ref,
            dst_ref=grad_buf.at[slot],
            send_sem=send_sem.at[0, d - 1],
            recv_sem=recv_sem.at[0, slot],
            device_id=device(peer),
            device_id_type=mesh_id,
        )

    def lat_copy(d, peer, chunk, slot):
        return pltpu.make_async_remote_copy(
            src_ref=lat_ref.at[chunk],
            dst_ref=lat_buf.at[slot],
            send_sem=send_sem.at[1, d - 1],
            recv_sem=recv_sem.at[1, slot],
            device_id=device(peer),
            device_id_type=mesh_id,
        )

    copies = []
    for d in range(1, count):
        target = (me + d) % count
        for copy in (lat_copy(d, target, target, me), grad_copy(d, target, me)):
            copy.start()
            copies.append(copy)
    grad_buf[me] = grad_ref[...]
    lat_buf[me] = lat_ref[me]
    for d in range(1, count):
        source = (me + count - d) % count
        lat_copy(d, source, source, source).wait_recv()
        grad_copy(d, source, source).wait_recv()
    for copy in copies:
        copy.wait_send()


def row_exchange(grad_send, lat_send):
    count = lat_send.shape[0]
    return pl.pallas_call(
        row_exchange_kernel,
        out_shape=(
            jax.ShapeDtypeStruct((count,) + grad_send.shape, grad_send.dtype),
            jax.ShapeDtypeStruct(lat_send.shape, lat_send.dtype),
        ),
        in_specs=[pl.BlockSpec(memory_space=pltpu.VMEM)] * 2,
        out_specs=(pl.BlockSpec(memory_space=pltpu.VMEM),) * 2,
        scratch_shapes=[
            pltpu.SemaphoreType.DMA((2, count - 1)),
            pltpu.SemaphoreType.DMA((2, count)),
        ],
        compiler_params=pltpu.CompilerParams(collective_id=1, has_side_effects=True),
    )(grad_send, lat_send)


def body(latents, grad_out, kernel):
    frames = grad_out.shape[1]
    height = grad_out.shape[2]
    width = grad_out.shape[3]
    channels = latents.shape[4]
    outputs = grad_out.shape[4]
    devices = lax.axis_size("dp") * lax.axis_size("tm") * lax.axis_size("rows")
    factor = float(devices * frames * height * width) ** (-0.5)
    slab_count = lax.axis_size("rows")

    near = with_halo(grad_out[0], "rows", 1, 1)
    later = shift_from(near, "tm", -1)
    grad_all = jnp.concatenate([near, later], axis=0)
    grad_all = jnp.pad(grad_all, ((0, 0), (0, 0), (1, 1), (0, 0)))
    patches = []
    for a in range(3):
        for i in range(3):
            for j in range(3):
                patches.append(
                    grad_all[2 - a : 2 - a + frames, 2 - i : 2 - i + height, 2 - j : 2 - j + width]
                )
    patches = jnp.stack(patches, axis=3).reshape(frames * height * width, 27, outputs)
    grad_up = lax.dot_general(
        patches,
        kernel.reshape(27, channels, outputs),
        (((1, 2), (0, 2)), ((), ())),
        preferred_element_type=jnp.float32,
    )
    pooled = grad_up.reshape(frames, height // 2, 2, width // 2, 2, channels).sum(axis=(2, 4))
    grad_latents = pooled.astype(jnp.bfloat16)[None]

    groups = lax.axis_size("dp") * lax.axis_size("tm")
    share = channels // devices
    earlier = shift_from(latents, "tm", 1)
    with_earlier = jnp.concatenate([earlier, latents], axis=1)[0, :, 0]
    lead = with_earlier.shape[:2]
    regrouped = with_earlier.reshape(lead + (groups, slab_count, share))
    regrouped = jnp.transpose(regrouped, (3, 0, 1, 2, 4))
    lat_send = regrouped.reshape(slab_count, -1, 128)
    grad_send = grad_out[0].reshape(frames * height * (width // 2), 2 * outputs)
    grad_buf, lat_buf = row_exchange(grad_send, lat_send)
    group_channels = groups * share
    owned = lat_buf.reshape(slab_count, lead[0], width // 2, group_channels)
    taps_a = jnp.stack([owned[:, a : a + frames] for a in range(3)], axis=0)

    whole = grad_buf.reshape(slab_count, frames, height, width // 2, 2 * outputs)
    whole = whole.astype(jnp.float32)
    top_row, bottom_row = whole[:, :, 0], whole[:, :, 1]
    zero = jnp.zeros_like(top_row[:1])
    rows_pooled = jnp.stack(
        [
            bottom_row + jnp.concatenate([top_row[1:], zero], axis=0),
            top_row + bottom_row,
            top_row + jnp.concatenate([zero, bottom_row[:-1]], axis=0),
        ],
        axis=2,
    )
    left, right = rows_pooled[..., :outputs], rows_pooled[..., outputs:]
    zero = jnp.zeros_like(left[:, :, :, :1])
    pooled_grad = jnp.stack(
        [
            right + jnp.concatenate([left[:, :, :, 1:], zero], axis=3),
            left + right,
            left + jnp.concatenate([zero, right[:, :, :, :-1]], axis=3),
        ],
        axis=4,
    )
    scaled = pooled_grad * 65537.0
    top = scaled - (scaled - pooled_grad)
    both = jnp.stack([top, pooled_grad - top], axis=0).astype(jnp.bfloat16)
    term = jnp.einsum(
        "arfsc,xrfisjo->caijxo", taps_a, both, preferred_element_type=jnp.float32
    )
    term = (term[..., 0, :] + term[..., 1, :]) * factor
    share_size = share * 27 * outputs
    term = term.reshape(groups, share_size // 128, 128)
    weight_grad = scatter_sum(term).reshape(share, 3, 3, 3, outputs)
    return (grad_latents, weight_grad)


def solution(mesh):
    in_specs = (P("dp", "tm", "rows", None, None), P("dp", "tm", "rows", None, None), P())
    out_specs = (P("dp", "tm", "rows", None, None), P(("dp", "tm", "rows"), None, None, None, None))
    return jax.shard_map(body, mesh=mesh, in_specs=in_specs, out_specs=out_specs, check_vma=False)
```

```python
import jax
import jax.numpy as jnp
from jax import lax
from jax.sharding import PartitionSpec as P
from jax.experimental import pallas as pl
from jax.experimental.pallas import tpu as pltpu


def shift_from(shard, axis, by):
    peers = lax.axis_size(axis)
    pairs = [(i, i + by) for i in range(peers) if 0 <= i + by < peers]
    return lax.ppermute(shard, axis, pairs)


def pool_pairs(values, dim):
    n = values.shape[dim] // 2
    pad = [(0, 0)] * values.ndim
    pad[dim] = (1, 1)
    ext = jnp.pad(values, pad)
    shape = values.shape
    shifted = ext.reshape(shape[:dim] + (n + 1, 2) + shape[dim + 1 :]).sum(axis=dim + 1)
    aligned = values.reshape(shape[:dim] + (n, 2) + shape[dim + 1 :]).sum(axis=dim + 1)
    out = [
        lax.slice_in_dim(shifted, 1, n + 1, axis=dim),
        aligned,
        lax.slice_in_dim(shifted, 0, n, axis=dim),
    ]
    return jnp.stack(out, axis=dim + 1)


def with_halo(block, axis, dim, width):
    count = lax.axis_size(axis)
    forward = [(i, i + 1) for i in range(count - 1)]
    backward = [(target, source) for source, target in forward]
    low = lax.ppermute(
        lax.slice_in_dim(block, block.shape[dim] - width, None, axis=dim), axis, forward
    )
    high = lax.ppermute(lax.slice_in_dim(block, 0, width, axis=dim), axis, backward)
    return jnp.concatenate([low, block, high], axis=dim)


def rows_group():
    def device(k):
        return (lax.axis_index("dp"), lax.axis_index("tm"), k)

    return lax.axis_size("rows"), lax.axis_index("rows"), device


def blocks_group():
    tm_size = lax.axis_size("tm")

    def device(k):
        return (k // tm_size, k % tm_size, lax.axis_index("rows"))

    me = lax.axis_index("dp") * tm_size + lax.axis_index("tm")
    return lax.axis_size("dp") * tm_size, me, device


def scatter_sum_kernel(term_ref, out_ref, slots, send_sem, recv_sem):
    count, me, device = rows_group()
    mesh_id = pl.DeviceIdType.MESH

    barrier = pltpu.get_barrier_semaphore()
    for d in range(1, count):
        pl.semaphore_signal(barrier, inc=1, device_id=device((me + d) % count), device_id_type=mesh_id)
    pl.semaphore_wait(barrier, count - 1)

    copies = []
    for d in range(1, count):
        target = (me + d) % count
        copy = pltpu.make_async_remote_copy(
            src_ref=term_ref.at[target],
            dst_ref=slots.at[me],
            send_sem=send_sem.at[d - 1],
            recv_sem=recv_sem.at[me],
            device_id=device(target),
            device_id_type=mesh_id,
        )
        copy.start()
        copies.append(copy)
    total = term_ref[me]
    for d in range(1, count):
        source = (me + count - d) % count
        incoming = pltpu.make_async_remote_copy(
            src_ref=term_ref.at[source],
            dst_ref=slots.at[source],
            send_sem=send_sem.at[d - 1],
            recv_sem=recv_sem.at[source],
            device_id=device(source),
            device_id_type=mesh_id,
        )
        incoming.wait_recv()
        total = total + slots[source]
    out_ref[...] = total
    for copy in copies:
        copy.wait_send()


def scatter_sum(term):
    count, rows, lanes = term.shape
    return pl.pallas_call(
        scatter_sum_kernel,
        out_shape=jax.ShapeDtypeStruct((rows, lanes), term.dtype),
        in_specs=[pl.BlockSpec(memory_space=pltpu.VMEM)],
        out_specs=pl.BlockSpec(memory_space=pltpu.VMEM),
        scratch_shapes=[
            pltpu.VMEM((count, rows, lanes), term.dtype),
            pltpu.SemaphoreType.DMA((count - 1,)),
            pltpu.SemaphoreType.DMA((count,)),
        ],
        compiler_params=pltpu.CompilerParams(collective_id=0, has_side_effects=True),
    )(term)


def block_exchange_kernel(grad_ref, lat_ref, grad_buf, lat_buf, send_sem, recv_sem):
    count, me, device = blocks_group()
    mesh_id = pl.DeviceIdType.MESH

    barrier = pltpu.get_barrier_semaphore()
    for d in range(1, count):
        pl.semaphore_signal(barrier, inc=1, device_id=device((me + d) % count), device_id_type=mesh_id)
    pl.semaphore_wait(barrier, count - 1)

    def grad_copy(d, peer, slot):
        return pltpu.make_async_remote_copy(
            src_ref=grad_ref,
            dst_ref=grad_buf.at[slot],
            send_sem=send_sem.at[0, d - 1],
            recv_sem=recv_sem.at[0, slot],
            device_id=device(peer),
            device_id_type=mesh_id,
        )

    def lat_copy(d, peer, chunk, slot):
        return pltpu.make_async_remote_copy(
            src_ref=lat_ref.at[chunk],
            dst_ref=lat_buf.at[slot],
            send_sem=send_sem.at[1, d - 1],
            recv_sem=recv_sem.at[1, slot],
            device_id=device(peer),
            device_id_type=mesh_id,
        )

    copies = []
    for d in range(1, count):
        target = (me + d) % count
        for copy in (lat_copy(d, target, target, me), grad_copy(d, target, me)):
            copy.start()
            copies.append(copy)
    grad_buf[me] = grad_ref[...]
    lat_buf[me] = lat_ref[me]
    for d in range(1, count):
        source = (me + count - d) % count
        lat_copy(d, source, source, source).wait_recv()
        grad_copy(d, source, source).wait_recv()
    for copy in copies:
        copy.wait_send()


def block_exchange(grad_send, lat_send):
    count = lat_send.shape[0]
    return pl.pallas_call(
        block_exchange_kernel,
        out_shape=(
            jax.ShapeDtypeStruct((count,) + grad_send.shape, grad_send.dtype),
            jax.ShapeDtypeStruct(lat_send.shape, lat_send.dtype),
        ),
        in_specs=[pl.BlockSpec(memory_space=pltpu.VMEM)] * 2,
        out_specs=(pl.BlockSpec(memory_space=pltpu.VMEM),) * 2,
        scratch_shapes=[
            pltpu.SemaphoreType.DMA((2, count - 1)),
            pltpu.SemaphoreType.DMA((2, count)),
        ],
        compiler_params=pltpu.CompilerParams(collective_id=1, has_side_effects=True),
    )(grad_send, lat_send)


def body(latents, grad_out, kernel):
    frames = grad_out.shape[1]
    height = grad_out.shape[2]
    width = grad_out.shape[3]
    channels = latents.shape[4]
    outputs = grad_out.shape[4]
    devices = lax.axis_size("dp") * lax.axis_size("tm") * lax.axis_size("rows")
    factor = float(devices * frames * height * width) ** (-0.5)
    slab_count = lax.axis_size("rows")

    near = with_halo(grad_out[0], "rows", 1, 1)
    later = shift_from(near, "tm", -1)
    grad_all = jnp.concatenate([near, later], axis=0)
    grad_all = jnp.pad(grad_all, ((0, 0), (0, 0), (1, 1), (0, 0)))
    patches = []
    for a in range(3):
        for i in range(3):
            for j in range(3):
                patches.append(
                    grad_all[2 - a : 2 - a + frames, 2 - i : 2 - i + height, 2 - j : 2 - j + width]
                )
    patches = jnp.stack(patches, axis=3).reshape(frames * height * width, 27, outputs)
    grad_up = lax.dot_general(
        patches,
        kernel.reshape(27, channels, outputs),
        (((1, 2), (0, 2)), ((), ())),
        preferred_element_type=jnp.float32,
    )
    pooled = grad_up.reshape(frames, height // 2, 2, width // 2, 2, channels).sum(axis=(2, 4))
    grad_latents = pooled.astype(jnp.bfloat16)[None]

    groups = lax.axis_size("dp") * lax.axis_size("tm")
    clips = lax.axis_size("dp")
    share = channels // devices
    group_channels = channels // groups
    lat_rows = with_halo(latents[0], "rows", 1, 1)
    lat_send = lat_rows.reshape(frames, 3, width // 2, groups, group_channels)
    lat_send = jnp.transpose(lat_send, (3, 0, 1, 2, 4)).reshape(groups, -1, 128)
    grad_send = grad_out[0].reshape(frames * height * (width // 2), 2 * outputs)
    grad_buf, lat_buf = block_exchange(grad_send, lat_send)
    all_frames = groups // clips * frames
    owned = lat_buf.reshape(clips, all_frames, 3, width // 2, group_channels)
    owned = jnp.pad(owned, ((0, 0), (2, 0), (0, 0), (0, 0), (0, 0)))
    taps = []
    for a in range(3):
        for i in range(3):
            per_row = [owned[:, a : a + all_frames, (r - 1 + i) // 2 + 1] for r in range(height)]
            taps.append(jnp.stack(per_row, axis=2))
    taps = jnp.stack(taps, axis=0)

    whole = grad_buf.reshape(clips, all_frames, height, width // 2, 2 * outputs)
    whole = whole.astype(jnp.float32)
    left, right = whole[..., :outputs], whole[..., outputs:]
    zero = jnp.zeros_like(left[:, :, :, :1])
    pooled_grad = jnp.stack(
        [
            right + jnp.concatenate([left[:, :, :, 1:], zero], axis=3),
            left + right,
            left + jnp.concatenate([zero, right[:, :, :, :-1]], axis=3),
        ],
        axis=4,
    )
    scaled = pooled_grad * 65537.0
    top = scaled - (scaled - pooled_grad)
    both = jnp.stack([top, pooled_grad - top], axis=0).astype(jnp.bfloat16)
    term = jnp.einsum(
        "kbflsc,xbflsjo->ckjxo", taps, both, preferred_element_type=jnp.float32
    )
    term = (term[..., 0, :] + term[..., 1, :]) * factor
    share_size = share * 27 * outputs
    term = term.reshape(slab_count, share_size // 128, 128)
    weight_grad = scatter_sum(term).reshape(share, 3, 3, 3, outputs)
    return (grad_latents, weight_grad)


def solution(mesh):
    in_specs = (P("dp", "tm", "rows", None, None), P("dp", "tm", "rows", None, None), P())
    out_specs = (P("dp", "tm", "rows", None, None), P(("dp", "tm", "rows"), None, None, None, None))
    return jax.shard_map(body, mesh=mesh, in_specs=in_specs, out_specs=out_specs, check_vma=False)
```

```python
import jax
import jax.numpy as jnp
from jax import lax
from jax.sharding import PartitionSpec as P
from jax.experimental import pallas as pl
from jax.experimental.pallas import tpu as pltpu


def shift_from(shard, axis, by):
    peers = lax.axis_size(axis)
    pairs = [(i, i + by) for i in range(peers) if 0 <= i + by < peers]
    return lax.ppermute(shard, axis, pairs)


def pool_pairs(values, dim):
    n = values.shape[dim] // 2
    pad = [(0, 0)] * values.ndim
    pad[dim] = (1, 1)
    ext = jnp.pad(values, pad)
    shape = values.shape
    shifted = ext.reshape(shape[:dim] + (n + 1, 2) + shape[dim + 1 :]).sum(axis=dim + 1)
    aligned = values.reshape(shape[:dim] + (n, 2) + shape[dim + 1 :]).sum(axis=dim + 1)
    out = [
        lax.slice_in_dim(shifted, 1, n + 1, axis=dim),
        aligned,
        lax.slice_in_dim(shifted, 0, n, axis=dim),
    ]
    return jnp.stack(out, axis=dim + 1)


def with_halo(block, axis, dim, width):
    count = lax.axis_size(axis)
    forward = [(i, i + 1) for i in range(count - 1)]
    backward = [(target, source) for source, target in forward]
    low = lax.ppermute(
        lax.slice_in_dim(block, block.shape[dim] - width, None, axis=dim), axis, forward
    )
    high = lax.ppermute(lax.slice_in_dim(block, 0, width, axis=dim), axis, backward)
    return jnp.concatenate([low, block, high], axis=dim)


def rows_group():
    def device(k):
        return (lax.axis_index("dp"), lax.axis_index("tm"), k)

    return lax.axis_size("rows"), lax.axis_index("rows"), device


def blocks_group():
    tm_size = lax.axis_size("tm")

    def device(k):
        return (k // tm_size, k % tm_size, lax.axis_index("rows"))

    me = lax.axis_index("dp") * tm_size + lax.axis_index("tm")
    return lax.axis_size("dp") * tm_size, me, device


def scatter_sum_kernel(term_ref, out_ref, half, partial, whole, sems):
    count, me, device = rows_group()
    ring = count // 2
    z, parity = me // 2, me % 2
    partner = me + 1 - 2 * parity
    mesh_id = pl.DeviceIdType.MESH
    send_half, recv_half, send_ring, recv_ring = sems

    barrier = pltpu.get_barrier_semaphore()
    pl.semaphore_signal(barrier, inc=1, device_id=device(partner), device_id_type=mesh_id)
    for d in range(1, ring):
        peer = ((z + d) % ring) * 2 + parity
        pl.semaphore_signal(barrier, inc=1, device_id=device(peer), device_id_type=mesh_id)
    pl.semaphore_wait(barrier, ring)

    def half_copy(m):
        return pltpu.make_async_remote_copy(
            src_ref=term_ref.at[2 * m + 1 - parity],
            dst_ref=half.at[m],
            send_sem=send_half.at[m],
            recv_sem=recv_half.at[m],
            device_id=device(partner),
            device_id_type=mesh_id,
        )

    copies = []
    for m in range(ring):
        copy = half_copy(m)
        copy.start()
        copies.append(copy)
    for m in range(ring):
        half_copy(m).wait_recv()
        partial[m] = term_ref[2 * m + parity] + half[m]

    def ring_copy(d, peer_z, slot):
        return pltpu.make_async_remote_copy(
            src_ref=partial.at[peer_z],
            dst_ref=whole.at[slot],
            send_sem=send_ring.at[d - 1],
            recv_sem=recv_ring.at[slot],
            device_id=device(peer_z * 2 + parity),
            device_id_type=mesh_id,
        )

    for d in range(1, ring):
        target = (z + d) % ring
        copy = ring_copy(d, target, z)
        copy.start()
        copies.append(copy)
    total = partial[z]
    for d in range(1, ring):
        source = (z + ring - d) % ring
        ring_copy(d, source, source).wait_recv()
        total = total + whole[source]
    out_ref[...] = total
    for copy in copies:
        copy.wait_send()


def scatter_sum(term):
    count, rows, lanes = term.shape
    ring = count // 2
    return pl.pallas_call(
        scatter_sum_kernel,
        out_shape=jax.ShapeDtypeStruct((rows, lanes), term.dtype),
        in_specs=[pl.BlockSpec(memory_space=pltpu.VMEM)],
        out_specs=pl.BlockSpec(memory_space=pltpu.VMEM),
        scratch_shapes=[
            pltpu.VMEM((ring, rows, lanes), term.dtype),
            pltpu.VMEM((ring, rows, lanes), term.dtype),
            pltpu.VMEM((ring, rows, lanes), term.dtype),
            (
                pltpu.SemaphoreType.DMA((ring,)),
                pltpu.SemaphoreType.DMA((ring,)),
                pltpu.SemaphoreType.DMA((ring - 1,)),
                pltpu.SemaphoreType.DMA((ring,)),
            ),
        ],
        compiler_params=pltpu.CompilerParams(collective_id=0, has_side_effects=True),
    )(term)


def block_exchange_kernel(grad_ref, lat_ref, grad_buf, lat_buf, send_sem, recv_sem):
    count, me, device = blocks_group()
    mesh_id = pl.DeviceIdType.MESH

    barrier = pltpu.get_barrier_semaphore()
    for d in range(1, count):
        pl.semaphore_signal(barrier, inc=1, device_id=device((me + d) % count), device_id_type=mesh_id)
    pl.semaphore_wait(barrier, count - 1)

    def grad_copy(d, peer, slot):
        return pltpu.make_async_remote_copy(
            src_ref=grad_ref,
            dst_ref=grad_buf.at[slot],
            send_sem=send_sem.at[0, d - 1],
            recv_sem=recv_sem.at[0, slot],
            device_id=device(peer),
            device_id_type=mesh_id,
        )

    def lat_copy(d, peer, chunk, slot):
        return pltpu.make_async_remote_copy(
            src_ref=lat_ref.at[chunk],
            dst_ref=lat_buf.at[slot],
            send_sem=send_sem.at[1, d - 1],
            recv_sem=recv_sem.at[1, slot],
            device_id=device(peer),
            device_id_type=mesh_id,
        )

    copies = []
    for d in range(1, count):
        target = (me + d) % count
        for copy in (lat_copy(d, target, target, me), grad_copy(d, target, me)):
            copy.start()
            copies.append(copy)
    grad_buf[me] = grad_ref[...]
    lat_buf[me] = lat_ref[me]
    for d in range(1, count):
        source = (me + count - d) % count
        lat_copy(d, source, source, source).wait_recv()
        grad_copy(d, source, source).wait_recv()
    for copy in copies:
        copy.wait_send()


def block_exchange(grad_send, lat_send):
    count = lat_send.shape[0]
    return pl.pallas_call(
        block_exchange_kernel,
        out_shape=(
            jax.ShapeDtypeStruct((count,) + grad_send.shape, grad_send.dtype),
            jax.ShapeDtypeStruct(lat_send.shape, lat_send.dtype),
        ),
        in_specs=[pl.BlockSpec(memory_space=pltpu.VMEM)] * 2,
        out_specs=(pl.BlockSpec(memory_space=pltpu.VMEM),) * 2,
        scratch_shapes=[
            pltpu.SemaphoreType.DMA((2, count - 1)),
            pltpu.SemaphoreType.DMA((2, count)),
        ],
        compiler_params=pltpu.CompilerParams(collective_id=1, has_side_effects=True),
    )(grad_send, lat_send)


def body(latents, grad_out, kernel):
    frames = grad_out.shape[1]
    height = grad_out.shape[2]
    width = grad_out.shape[3]
    channels = latents.shape[4]
    outputs = grad_out.shape[4]
    devices = lax.axis_size("dp") * lax.axis_size("tm") * lax.axis_size("rows")
    factor = float(devices * frames * height * width) ** (-0.5)
    slab_count = lax.axis_size("rows")

    near = with_halo(grad_out[0], "rows", 1, 1)
    later = shift_from(near, "tm", -1)
    grad_all = jnp.concatenate([near, later], axis=0)
    grad_all = jnp.pad(grad_all, ((0, 0), (0, 0), (1, 1), (0, 0)))
    patches = []
    for a in range(3):
        for i in range(3):
            for j in range(3):
                patches.append(
                    grad_all[2 - a : 2 - a + frames, 2 - i : 2 - i + height, 2 - j : 2 - j + width]
                )
    patches = jnp.stack(patches, axis=3).reshape(frames * height * width, 27, outputs)
    grad_up = lax.dot_general(
        patches,
        kernel.reshape(27, channels, outputs),
        (((1, 2), (0, 2)), ((), ())),
        preferred_element_type=jnp.float32,
    )
    pooled = grad_up.reshape(frames, height // 2, 2, width // 2, 2, channels).sum(axis=(2, 4))
    grad_latents = pooled.astype(jnp.bfloat16)[None]

    groups = lax.axis_size("dp") * lax.axis_size("tm")
    clips = lax.axis_size("dp")
    share = channels // devices
    group_channels = channels // groups
    lat_rows = with_halo(latents[0], "rows", 1, 1)
    lat_send = lat_rows.reshape(frames, 3, width // 2, groups, group_channels)
    lat_send = jnp.transpose(lat_send, (3, 0, 1, 2, 4)).reshape(groups, -1, 128)
    grad_send = grad_out[0].reshape(frames * height * (width // 2), 2 * outputs)
    grad_buf, lat_buf = block_exchange(grad_send, lat_send)
    all_frames = groups // clips * frames
    owned = lat_buf.reshape(clips, all_frames, 3, width // 2, group_channels)
    owned = jnp.pad(owned, ((0, 0), (2, 0), (0, 0), (0, 0), (0, 0)))
    taps = []
    for a in range(3):
        for i in range(3):
            per_row = [owned[:, a : a + all_frames, (r - 1 + i) // 2 + 1] for r in range(height)]
            taps.append(jnp.stack(per_row, axis=2))
    taps = jnp.stack(taps, axis=0)

    whole = grad_buf.reshape(clips, all_frames, height, width // 2, 2 * outputs)
    whole = whole.astype(jnp.float32)
    left, right = whole[..., :outputs], whole[..., outputs:]
    zero = jnp.zeros_like(left[:, :, :, :1])
    pooled_grad = jnp.stack(
        [
            right + jnp.concatenate([left[:, :, :, 1:], zero], axis=3),
            left + right,
            left + jnp.concatenate([zero, right[:, :, :, :-1]], axis=3),
        ],
        axis=4,
    )
    scaled = pooled_grad * 65537.0
    top = scaled - (scaled - pooled_grad)
    both = jnp.stack([top, pooled_grad - top], axis=0).astype(jnp.bfloat16)
    term = jnp.einsum(
        "kbflsc,xbflsjo->ckjxo", taps, both, preferred_element_type=jnp.float32
    )
    term = (term[..., 0, :] + term[..., 1, :]) * factor
    share_size = share * 27 * outputs
    term = term.reshape(slab_count, share_size // 128, 128)
    weight_grad = scatter_sum(term).reshape(share, 3, 3, 3, outputs)
    return (grad_latents, weight_grad)


def solution(mesh):
    in_specs = (P("dp", "tm", "rows", None, None), P("dp", "tm", "rows", None, None), P())
    out_specs = (P("dp", "tm", "rows", None, None), P(("dp", "tm", "rows"), None, None, None, None))
    return jax.shard_map(body, mesh=mesh, in_specs=in_specs, out_specs=out_specs, check_vma=False)
```

```python
import jax
import jax.numpy as jnp
from jax import lax
from jax.sharding import PartitionSpec as P
from jax.experimental import pallas as pl
from jax.experimental.pallas import tpu as pltpu


def shift_from(shard, axis, by):
    peers = lax.axis_size(axis)
    pairs = [(i, i + by) for i in range(peers) if 0 <= i + by < peers]
    return lax.ppermute(shard, axis, pairs)


def pool_pairs(values, dim):
    n = values.shape[dim] // 2
    pad = [(0, 0)] * values.ndim
    pad[dim] = (1, 1)
    ext = jnp.pad(values, pad)
    shape = values.shape
    shifted = ext.reshape(shape[:dim] + (n + 1, 2) + shape[dim + 1 :]).sum(axis=dim + 1)
    aligned = values.reshape(shape[:dim] + (n, 2) + shape[dim + 1 :]).sum(axis=dim + 1)
    out = [
        lax.slice_in_dim(shifted, 1, n + 1, axis=dim),
        aligned,
        lax.slice_in_dim(shifted, 0, n, axis=dim),
    ]
    return jnp.stack(out, axis=dim + 1)


def with_halo(block, axis, dim, width):
    count = lax.axis_size(axis)
    forward = [(i, i + 1) for i in range(count - 1)]
    backward = [(target, source) for source, target in forward]
    low = lax.ppermute(
        lax.slice_in_dim(block, block.shape[dim] - width, None, axis=dim), axis, forward
    )
    high = lax.ppermute(lax.slice_in_dim(block, 0, width, axis=dim), axis, backward)
    return jnp.concatenate([low, block, high], axis=dim)


def rows_group():
    def device(k):
        return (lax.axis_index("dp"), lax.axis_index("tm"), k)

    return lax.axis_size("rows"), lax.axis_index("rows"), device


def blocks_group():
    tm_size = lax.axis_size("tm")

    def device(k):
        return (k // tm_size, k % tm_size, lax.axis_index("rows"))

    me = lax.axis_index("dp") * tm_size + lax.axis_index("tm")
    return lax.axis_size("dp") * tm_size, me, device


def scatter_sum_kernel(term_ref, out_ref, slots, send_sem, recv_sem):
    count, me, device = rows_group()
    mesh_id = pl.DeviceIdType.MESH

    barrier = pltpu.get_barrier_semaphore()
    for d in range(1, count):
        pl.semaphore_signal(barrier, inc=1, device_id=device((me + d) % count), device_id_type=mesh_id)
    pl.semaphore_wait(barrier, count - 1)

    copies = []
    for d in range(1, count):
        target = (me + d) % count
        copy = pltpu.make_async_remote_copy(
            src_ref=term_ref.at[target],
            dst_ref=slots.at[me],
            send_sem=send_sem.at[d - 1],
            recv_sem=recv_sem.at[me],
            device_id=device(target),
            device_id_type=mesh_id,
        )
        copy.start()
        copies.append(copy)
    total = term_ref[me]
    for d in range(1, count):
        source = (me + count - d) % count
        incoming = pltpu.make_async_remote_copy(
            src_ref=term_ref.at[source],
            dst_ref=slots.at[source],
            send_sem=send_sem.at[d - 1],
            recv_sem=recv_sem.at[source],
            device_id=device(source),
            device_id_type=mesh_id,
        )
        incoming.wait_recv()
        total = total + slots[source]
    out_ref[...] = total
    for copy in copies:
        copy.wait_send()


def scatter_sum(term):
    count, rows, lanes = term.shape
    return pl.pallas_call(
        scatter_sum_kernel,
        out_shape=jax.ShapeDtypeStruct((rows, lanes), term.dtype),
        in_specs=[pl.BlockSpec(memory_space=pltpu.VMEM)],
        out_specs=pl.BlockSpec(memory_space=pltpu.VMEM),
        scratch_shapes=[
            pltpu.VMEM((count, rows, lanes), term.dtype),
            pltpu.SemaphoreType.DMA((count - 1,)),
            pltpu.SemaphoreType.DMA((count,)),
        ],
        compiler_params=pltpu.CompilerParams(collective_id=0, has_side_effects=True),
    )(term)


def block_exchange_kernel(grad_ref, lat_ref, grad_buf, lat_buf, send_sem, recv_sem):
    count, me, device = blocks_group()
    mesh_id = pl.DeviceIdType.MESH

    barrier = pltpu.get_barrier_semaphore()
    for d in range(1, count):
        pl.semaphore_signal(barrier, inc=1, device_id=device((me + d) % count), device_id_type=mesh_id)
    pl.semaphore_wait(barrier, count - 1)

    def grad_copy(d, peer, slot):
        return pltpu.make_async_remote_copy(
            src_ref=grad_ref,
            dst_ref=grad_buf.at[slot],
            send_sem=send_sem.at[0, d - 1],
            recv_sem=recv_sem.at[0, slot],
            device_id=device(peer),
            device_id_type=mesh_id,
        )

    def lat_copy(d, peer, chunk, slot):
        return pltpu.make_async_remote_copy(
            src_ref=lat_ref.at[chunk],
            dst_ref=lat_buf.at[slot],
            send_sem=send_sem.at[1, d - 1],
            recv_sem=recv_sem.at[1, slot],
            device_id=device(peer),
            device_id_type=mesh_id,
        )

    copies = []
    for d in range(1, count):
        target = (me + d) % count
        copy = grad_copy(d, target, me)
        copy.start()
        copies.append(copy)
    for d in range(1, count):
        target = (me + d) % count
        copy = lat_copy(d, target, target, me)
        copy.start()
        copies.append(copy)
    grad_buf[me] = grad_ref[...]
    lat_buf[me] = lat_ref[me]
    for d in range(1, count):
        source = (me + count - d) % count
        lat_copy(d, source, source, source).wait_recv()
        grad_copy(d, source, source).wait_recv()
    for copy in copies:
        copy.wait_send()


def block_exchange(grad_send, lat_send):
    count = lat_send.shape[0]
    return pl.pallas_call(
        block_exchange_kernel,
        out_shape=(
            jax.ShapeDtypeStruct((count,) + grad_send.shape, grad_send.dtype),
            jax.ShapeDtypeStruct(lat_send.shape, lat_send.dtype),
        ),
        in_specs=[pl.BlockSpec(memory_space=pltpu.VMEM)] * 2,
        out_specs=(pl.BlockSpec(memory_space=pltpu.VMEM),) * 2,
        scratch_shapes=[
            pltpu.SemaphoreType.DMA((2, count - 1)),
            pltpu.SemaphoreType.DMA((2, count)),
        ],
        compiler_params=pltpu.CompilerParams(collective_id=1, has_side_effects=True),
    )(grad_send, lat_send)


def body(latents, grad_out, kernel):
    frames = grad_out.shape[1]
    height = grad_out.shape[2]
    width = grad_out.shape[3]
    channels = latents.shape[4]
    outputs = grad_out.shape[4]
    devices = lax.axis_size("dp") * lax.axis_size("tm") * lax.axis_size("rows")
    factor = float(devices * frames * height * width) ** (-0.5)
    slab_count = lax.axis_size("rows")

    near = with_halo(grad_out[0], "rows", 1, 1)
    later = shift_from(near, "tm", -1)
    grad_all = jnp.concatenate([near, later], axis=0)
    grad_all = jnp.pad(grad_all, ((0, 0), (0, 0), (1, 1), (0, 0)))
    patches = []
    for a in range(3):
        for i in range(3):
            for j in range(3):
                patches.append(
                    grad_all[2 - a : 2 - a + frames, 2 - i : 2 - i + height, 2 - j : 2 - j + width]
                )
    patches = jnp.stack(patches, axis=3).reshape(frames * height * width, 27, outputs)
    grad_up = lax.dot_general(
        patches,
        kernel.reshape(27, channels, outputs),
        (((1, 2), (0, 2)), ((), ())),
        preferred_element_type=jnp.float32,
    )
    pooled = grad_up.reshape(frames, height // 2, 2, width // 2, 2, channels).sum(axis=(2, 4))
    grad_latents = pooled.astype(jnp.bfloat16)[None]

    groups = lax.axis_size("dp") * lax.axis_size("tm")
    clips = lax.axis_size("dp")
    share = channels // devices
    group_channels = channels // groups
    lat_rows = with_halo(latents[0], "rows", 1, 1)
    lat_send = lat_rows.reshape(frames, 3, width // 2, groups, group_channels)
    lat_send = jnp.transpose(lat_send, (3, 0, 1, 2, 4)).reshape(groups, -1, 128)
    grad_send = grad_out[0].reshape(frames * height * (width // 2), 2 * outputs)
    grad_buf, lat_buf = block_exchange(grad_send, lat_send)
    all_frames = groups // clips * frames
    owned = lat_buf.reshape(clips, all_frames, 3, width // 2, group_channels)
    owned = jnp.pad(owned, ((0, 0), (2, 0), (0, 0), (0, 0), (0, 0)))
    taps = []
    for a in range(3):
        for i in range(3):
            per_row = [owned[:, a : a + all_frames, (r - 1 + i) // 2 + 1] for r in range(height)]
            taps.append(jnp.stack(per_row, axis=2))
    taps = jnp.stack(taps, axis=0)

    whole = grad_buf.reshape(clips, all_frames, height, width // 2, 2 * outputs)
    whole = whole.astype(jnp.float32)
    left, right = whole[..., :outputs], whole[..., outputs:]
    zero = jnp.zeros_like(left[:, :, :, :1])
    pooled_grad = jnp.stack(
        [
            right + jnp.concatenate([left[:, :, :, 1:], zero], axis=3),
            left + right,
            left + jnp.concatenate([zero, right[:, :, :, :-1]], axis=3),
        ],
        axis=4,
    )
    scaled = pooled_grad * 65537.0
    top = scaled - (scaled - pooled_grad)
    both = jnp.stack([top, pooled_grad - top], axis=0).astype(jnp.bfloat16)
    term = jnp.einsum(
        "kbflsc,xbflsjo->ckjxo", taps, both, preferred_element_type=jnp.float32
    )
    term = (term[..., 0, :] + term[..., 1, :]) * factor
    share_size = share * 27 * outputs
    term = term.reshape(slab_count, share_size // 128, 128)
    weight_grad = scatter_sum(term).reshape(share, 3, 3, 3, outputs)
    return (grad_latents, weight_grad)


def solution(mesh):
    in_specs = (P("dp", "tm", "rows", None, None), P("dp", "tm", "rows", None, None), P())
    out_specs = (P("dp", "tm", "rows", None, None), P(("dp", "tm", "rows"), None, None, None, None))
    return jax.shard_map(body, mesh=mesh, in_specs=in_specs, out_specs=out_specs, check_vma=False)
```
